256 devices in a mesh: tm: 64 (over x, z, core), mp: 4 (over y).
Axes of the slice: x: 4, y: 4, z: 8, core: 2. Of those that a mesh axis runs over, the one named last changes fastest.
Arguments:
- features: bfloat16 [2048, 2048], P('tm'), may hold values from -6 to 6
- w_in: bfloat16 [2048, 4096], P(None, 'mp'), may hold values from -0.125 to 0.125
- b_in: float32 [4096], P('mp'), may hold values from -5 to 5
- output_weight: bfloat16 [4096, 256], P('mp'), may hold values from -0.09375 to 0.09375
- final_offset_entries: float32 [256], replicated, may hold values from -3 to 3
- transition: float32 [256, 256], replicated, may hold values from -1 to 1
- gains: float32 [2048, 256], P('tm'), may hold values from 0 to 1
- smooth_gains: float32 [2048, 256], P('tm'), may hold values from 0 to 1
Outputs:
- filtered: float32 [2048, 256], P(('tm', 'mp'))
- smoothed: float32 [2048, 256], P(('tm', 'mp'))
The draws below stay inside these ranges and needn't reach their ends.
All inputs are finite; a program needn't handle non-finite values.
Results may differ from the reference program's by a relative error of at most 0.0021.
Values sent between devices are 32-bit elements; how exact they have to be, the bound alone decides.
No kernel may reach another device: no remote copies, remote signals or barrier semaphores. Data moves between devices by JAX's collectives and lax.ppermute only.
A program may use at most 128 MiB of HBM per device.

```python
import math
import jax
import jax.numpy as jnp
from jax import lax

GRID = 256
HID_UNITS = 4096
FR_DEV = 32
FEATURES = 2048
TRACK_SNAPSHOTS = 2048


def retention_field(key):
    sampler_seeds = jax.random.split(key, 5)
    low = math.log(0.1 / TRACK_SNAPSHOTS)
    high = math.log(1.0 / 30.0)
    channel = jnp.exp(jax.random.uniform(sampler_seeds[0], (1, GRID), jnp.float32, low, high))
    blocks = jnp.exp(jax.random.uniform(sampler_seeds[1], (TRACK_SNAPSHOTS // FR_DEV, 1), jnp.float32, -0.7, 0.7))
    blocks = jnp.repeat(blocks, FR_DEV, axis=0)
    rough = jax.random.uniform(sampler_seeds[2], (TRACK_SNAPSHOTS, GRID), jnp.float32, 0.5, 1.5)
    forgetting_factor = channel * blocks * rough
    cluster_extent = jax.random.bernoulli(sampler_seeds[3], 4.0 / TRACK_SNAPSHOTS, (TRACK_SNAPSHOTS, 1)).astype(jnp.float32)
    doubling_height = jax.random.uniform(sampler_seeds[4], (1, GRID), jnp.float32, 0.2, 0.5)
    return jnp.exp(-forgetting_factor) * (1.0 - cluster_extent * doubling_height)


def draw_transition(key, part):
    raw = jax.random.normal(jax.random.fold_in(key, 5), (GRID, GRID), jnp.float32) * (0.6 / math.sqrt(GRID))
    skew = raw - raw.T
    eye = jnp.eye(GRID, dtype=jnp.float32)
    return jnp.linalg.solve(eye - skew, eye + skew).astype(jnp.float32)


def draw_gains(key, part):
    return (1.0 - retention_field(jax.random.fold_in(key, 11))).astype(jnp.float32)


def draw_smooth_gains(key, part):
    return retention_field(jax.random.fold_in(key, 23)).astype(jnp.float32)


def block_levels(key, extent, cuts, low, high):
    level = 1.0
    for dim, parts in cuts:
        draws = jax.random.uniform(jax.random.fold_in(jax.random.fold_in(key, 6), dim), (parts,), jnp.float32, low / len(cuts), high / len(cuts))
        level = level * jnp.repeat(jnp.exp(draws), extent[dim] // parts).reshape((-1,) + (1,) * (len(extent) - 1 - dim))
    return level


def scatter_about(own_key, extent, deviation, limit, cuts=(), kind=jnp.bfloat16):
    result = jax.random.normal(own_key, extent, jnp.float32) * deviation
    if len(cuts) > 0:
        result = block_levels(own_key, extent, cuts, -0.22, 0.18) * result
    return jnp.clip(result, min=-limit, max=limit).astype(kind)


def setup_inputs(seed: int = 0) -> dict:
    key_list = jax.random.split(jax.random.key(seed), 9)
    return {
        "features": scatter_about(key_list[0], (TRACK_SNAPSHOTS, FEATURES), 1.0, 6.0, ((0, 64),)),
        "w_in": scatter_about(key_list[1], (FEATURES, HID_UNITS), FEATURES ** -0.5, 0.125, ((1, 4),)),
        "b_in": scatter_about(key_list[2], (HID_UNITS,), 1.0, 5.0, ((0, 4),), jnp.float32),
        "output_weight": scatter_about(key_list[3], (HID_UNITS, GRID), HID_UNITS ** -0.5, 0.09375, ((0, 4),)),
        "final_offset_entries": scatter_about(key_list[4], (GRID,), 0.5, 3.0, (), jnp.float32),
        "transition": draw_transition(jax.random.fold_in(key_list[8], 71), 0),
        "gains": draw_gains(jax.random.fold_in(key_list[8], 71), 0),
        "smooth_gains": draw_smooth_gains(jax.random.fold_in(key_list[8], 71), 0),
    }


def reference(features, w_in, b_in, output_weight, final_offset_entries, transition, gains, smooth_gains):
    pre = jnp.dot(features.astype(jnp.float32), w_in.astype(jnp.float32), preferred_element_type=jnp.float32) + b_in
    hidden_layer = jax.nn.gelu(pre, approximate=True).astype(jnp.bfloat16)
    measured_values = jnp.dot(hidden_layer.astype(jnp.float32), output_weight.astype(jnp.float32), preferred_element_type=jnp.float32) + final_offset_entries

    def forward_pass(state, current_row):
        gain_vector, measurement_row = current_row
        moved_state = jnp.dot(transition, state, precision=lax.Precision.HIGHEST)
        fresh_value = (1.0 - gain_vector) * moved_state + gain_vector * measurement_row
        return (fresh_value, fresh_value)
    start_index = jnp.zeros((GRID,), jnp.float32)
    unused_item, filtered = lax.scan(forward_pass, start_index, (gains, measured_values))
    predicted = jnp.dot(filtered, transition.T, precision=lax.Precision.HIGHEST)
    weight = smooth_gains.at[-1].set(0.0)

    def backward(state, current_row):
        weight_row, filt_row, pred_row = current_row
        fresh_value = filt_row + weight_row * (state - pred_row)
        return (fresh_value, fresh_value)
    unused_item, smoothed = lax.scan(backward, start_index, (weight, filtered, predicted), reverse=True)
    return (filtered, smoothed)
```

```python
import jax
import jax.numpy as jnp
from jax import lax
from jax.experimental import pallas as pl
from jax.experimental.pallas import tpu as pltpu
from jax.sharding import Mesh
from jax.sharding import PartitionSpec as P

TM = ("x", "z", "c")
F32, BF16 = jnp.float32, jnp.bfloat16
SUB = 8
VEC = 8


def pieces(a):
    high = a.astype(BF16)
    return high, (a - high.astype(F32)).astype(BF16)


def left(a):
    high, low = pieces(a)
    return jnp.concatenate([high, low, high], axis=1)


def right(b):
    high, low = pieces(b)
    return jnp.concatenate([high, high, low], axis=0)


def times(a, b3):
    return jnp.dot(left(a), b3, preferred_element_type=F32)


def each(ref, t, chains):
    return jnp.concatenate([ref[SUB * j + t : SUB * j + t + 1, :] for j in range(chains)], axis=0)


def block_kernel(gains_ref, transition_ref, chain_ref, prefix_ref):
    grid = transition_ref.shape[0]
    chains = chain_ref.shape[0]
    flipped = transition_ref[...].T
    step = right(flipped)
    for j in range(chains):
        chain_ref[j] = flipped * (1.0 - gains_ref[SUB * j : SUB * j + 1, :])
    for t in range(1, SUB):
        for part in range(2):
            own = range(part * chains // 2, (part + 1) * chains // 2)
            moved = times(jnp.concatenate([chain_ref[j] for j in own], axis=0), step)
            for n, j in enumerate(own):
                row = SUB * j + t
                keep = 1.0 - gains_ref[row : row + 1, :]
                chain_ref[j] = moved[n * grid : (n + 1) * grid] * keep
    prefix_ref[0] = chain_ref[0]
    for j in range(1, chains):
        prefix_ref[j] = times(prefix_ref[j - 1], right(chain_ref[j]))


def response_kernel(
    partial_ref, offset_ref, gains_ref, transition_ref, chain_ref, prefix_ref,
    whole_ref, drive_ref, start_ref,
):
    chains, grid = chain_ref.shape[0], transition_ref.shape[0]
    step = right(transition_ref[...].T)
    measured = partial_ref[0] + partial_ref[1] + partial_ref[2] + partial_ref[3]
    drive_ref[...] = gains_ref[...] * (measured + offset_ref[...])
    state = each(drive_ref, 0, chains)
    for t in range(1, SUB):
        keep = 1.0 - each(gains_ref, t, chains)
        state = times(state, step) * keep + each(drive_ref, t, chains)
    start_ref[...] = jnp.zeros_like(start_ref)
    carried = state[0:1]
    for j in range(1, chains):
        start_ref[j : j + 1, :] = carried
        carried = times(carried, right(chain_ref[j])) + state[j : j + 1]
    whole_ref[0:grid, :] = prefix_ref[chains - 1]
    whole_ref[grid:, :] = jnp.concatenate([carried, jnp.zeros((VEC - 1, grid), F32)], axis=0)


def after(earlier, later):
    grid = later.shape[1]
    added = jnp.concatenate([jnp.zeros((grid, grid), F32), later[grid:]], axis=0)
    return times(earlier, right(later[:grid])) + added


def pair_kernel(both_ref, whole_ref):
    whole_ref[...] = after(both_ref[0], both_ref[1])


def quad_kernel(place_ref, own_ref, others_ref, whole_ref, before_ref, held):
    grid = own_ref.shape[1]
    half = grid // 2
    place = place_ref[0]
    held[0] = own_ref[...]
    for s in range(1, 4):
        held[s, 0:half, :] = others_ref[0, s - 1, 0:half, :]
        held[s, half:grid, :] = others_ref[1, s - 1, 0:half, :]
        held[s, grid:, :] = others_ref[0, s - 1, half:, :]
    before_ref[...] = jnp.zeros_like(before_ref)
    total = held[lax.rem(place, 4)]
    for i in range(1, 4):
        @pl.when(place == i)
        def _(total=total):
            before_ref[...] = total
        total = after(total, held[lax.rem(place - i + 4, 4)])
    whole_ref[...] = total


def advance(state, whole):
    grid = whole.shape[1]
    return times(state, right(whole[:grid])) + whole[grid : grid + 1]


def hop_kernel(state_ref, whole_ref, out_ref):
    out_ref[...] = advance(state_ref[...], whole_ref[...])


def final_kernel(
    place_ref, state_ref, quad_ref, pair_ref, core_ref, prefix_ref, start_ref, drive_ref,
    gains_ref, smooth_ref, transition_ref,
    filtered_ref, weight_ref, value_ref, send_ref, found, scan_d, scan_v,
):
    chains = prefix_ref.shape[0]
    frames, grid = drive_ref.shape
    quad, pair, core, part, last = (place_ref[k] for k in range(5))
    step = right(transition_ref[...].T)
    state = state_ref[...]
    state = jnp.where(quad > 0, advance(state, quad_ref[...]), state)
    state = jnp.where(pair > 0, advance(state, pair_ref[0]), state)
    state = jnp.where(core > 0, advance(state, core_ref[0]), state)
    rows = [state[0:1]]
    for j in range(1, chains):
        rows.append(times(state, right(prefix_ref[j - 1]))[0:1] + start_ref[j : j + 1, :])
    now = jnp.concatenate(rows, axis=0)
    for t in range(SUB):
        keep = 1.0 - each(gains_ref, t, chains)
        now = times(now, step) * keep + each(drive_ref, t, chains)
        for j in range(chains):
            found[SUB * j + t : SUB * j + t + 1, :] = now[j : j + 1]
    weight = smooth_ref[...]
    row = lax.broadcasted_iota(jnp.int32, (frames, grid), 0)
    weight = jnp.where((row == frames - 1) & (last > 0), 0.0, weight)
    value = found[...] - weight * times(found[...], step)
    d, v = weight[frames - 1 : frames], value[frames - 1 : frames]
    scan_d[frames - 1 : frames, :] = d
    scan_v[frames - 1 : frames, :] = v
    for t in range(frames - 2, -1, -1):
        v = weight[t : t + 1] * v + value[t : t + 1]
        d = weight[t : t + 1] * d
        scan_d[t : t + 1, :] = d
        scan_v[t : t + 1, :] = v
    share = filtered_ref.shape[0]
    mine = pl.ds(pl.multiple_of(part * share, share), share)
    filtered_ref[...] = found[mine, :]
    weight_ref[...] = scan_d[mine, :]
    value_ref[...] = scan_v[mine, :]
    send_ref[...] = jnp.broadcast_to(jnp.concatenate([d, v], axis=1), send_ref.shape)


def smooth_kernel(place_ref, got_ref, weight_ref, value_ref, smoothed_ref):
    blocks = got_ref.shape[0]
    grid = weight_ref.shape[1]
    here = place_ref[5]
    row = lax.broadcasted_iota(jnp.int32, (blocks, grid), 0)
    d = jnp.where(row > here, got_ref[:, :grid], 1.0)
    v = jnp.where(row > here, got_ref[:, grid:], 0.0)
    later = jnp.zeros((1, grid), F32)
    for k in range(blocks - 1, -1, -1):
        later = d[k : k + 1] * later + v[k : k + 1]
    smoothed_ref[...] = weight_ref[...] * later + value_ref[...]


def shape(*dims):
    return jax.ShapeDtypeStruct(dims, F32)


V = pl.BlockSpec(memory_space=pltpu.VMEM)
S = pl.BlockSpec(memory_space=pltpu.SMEM)
ROOM = pltpu.CompilerParams(vmem_limit_bytes=48 << 20)


def call(kernel, ins, outs, out_shape, scratch=()):
    return pl.pallas_call(
        kernel, in_specs=ins, out_specs=outs, out_shape=out_shape,
        scratch_shapes=list(scratch), compiler_params=ROOM,
    )


def on_device(
    features, w_in, b_in, output_weight, final_offset_entries, transition, gains, smooth_gains
):
    frames, grid = gains.shape
    chains = frames // SUB
    rows = grid + VEC
    x, z, c, part = (lax.axis_index(a) for a in ("x", "z", "c", "y"))
    blocks = lax.axis_size(TM)
    here = lax.axis_index(TM)
    quad = z // 2
    last = (here == blocks - 1).astype(jnp.int32)
    place = jnp.stack([quad, z % 2, c, part, last, here]).astype(jnp.int32)

    pre = jnp.dot(features, w_in, preferred_element_type=F32) + b_in
    hidden = jax.nn.gelu(pre, approximate=True).astype(BF16)
    partial = jnp.dot(hidden, output_weight, preferred_element_type=F32)
    parts = lax.axis_size("y")
    partials = lax.all_to_all(
        jnp.broadcast_to(partial, (parts, frames, grid)), "y", 0, 0, tiled=True
    )

    chain, prefix = call(
        block_kernel, [V, V], [V, V],
        [shape(chains, grid, grid), shape(chains, grid, grid)],
    )(gains, transition)
    whole, drive, start = call(
        response_kernel, [V] * 6, [V] * 3,
        [shape(rows, grid), shape(frames, grid), shape(VEC, grid)],
    )(partials, final_offset_entries[None], gains, transition, chain, prefix)

    cores = lax.all_gather(whole, "c")
    pair = call(pair_kernel, [V], V, shape(rows, grid))(cores)
    pairs = lax.all_gather(
        pair, "z", axis_index_groups=[[2 * k, 2 * k + 1] for k in range(4)]
    )
    four = call(pair_kernel, [V], V, shape(rows, grid))(pairs)
    half = grid // 2
    mine = jnp.concatenate(
        [lax.dynamic_slice_in_dim(four, c * half, half, 0), four[grid:]], axis=0
    )
    others = jnp.stack(
        [
            lax.ppermute(mine, "z", [(k, (k + 2 * s) % 8) for k in range(8)])
            for s in range(1, 4)
        ]
    )
    others = lax.all_gather(others, "c")
    group, before = call(
        quad_kernel, [S, V, V], [V, V], [shape(rows, grid), shape(rows, grid)],
        [pltpu.VMEM((4, rows, grid), F32)],
    )(place, four, others)

    forward = [(k, k + 1) for k in range(3)]
    state = lax.ppermute(group[grid:], "x", forward)
    for _ in range(2):
        state = call(hop_kernel, [V, V], V, shape(VEC, grid))(state, group)
        state = lax.ppermute(state, "x", forward)

    share = frames // parts
    filtered, weight, value, send = call(
        final_kernel, [S] + [V] * 10, [V] * 4,
        [shape(share, grid)] * 3 + [shape(blocks, 2 * grid)],
        [pltpu.VMEM((frames, grid), F32)] * 3,
    )(place, state, before, pairs, cores, prefix, start, drive, gains, smooth_gains, transition)
    got = lax.all_to_all(send, TM, 0, 0, tiled=True)
    smoothed = call(smooth_kernel, [S, V, V, V], V, shape(share, grid))(
        place, got, weight, value
    )
    return filtered, smoothed


def solution(mesh):
    torus = Mesh(mesh.devices.reshape(4, 8, 2, mesh.shape["mp"]), ("x", "z", "c", "y"))
    return jax.shard_map(
        on_device,
        mesh=torus,
        in_specs=(
            P(TM, None), P(None, "y"), P("y"), P("y", None), P(), P(), P(TM, None), P(TM, None),
        ),
        out_specs=(P((*TM, "y"), None), P((*TM, "y"), None)),
        check_vma=False,
    )
```

```python
import functools

import jax
import jax.numpy as jnp
from jax import lax
from jax.experimental import pallas as pl
from jax.experimental.pallas import tpu as pltpu
from jax.sharding import Mesh
from jax.sharding import PartitionSpec as P

TM = ("x", "z", "c")
F32, BF16 = jnp.float32, jnp.bfloat16
SUB = 8
VEC = 8


def pieces(a):
    high = a.astype(BF16)
    return high, (a - high.astype(F32)).astype(BF16)


def left(a):
    high, low = pieces(a)
    return jnp.concatenate([high, low, high], axis=1)


def right(b):
    high, low = pieces(b)
    return jnp.concatenate([high, high, low], axis=0)


def times(a, b3):
    return jnp.dot(left(a), b3, preferred_element_type=F32)


def each(ref, t, chains):
    return jnp.concatenate([ref[SUB * j + t : SUB * j + t + 1, :] for j in range(chains)], axis=0)


def bit(level):
    if level == 0:
        return lax.axis_index("c")
    if level < 4:
        return (lax.axis_index("z") >> (level - 1)) & 1
    return (lax.axis_index("x") >> (level - 4)) & 1


def network_kernel(
    features_hbm, w_in_hbm, b_in_hbm, out_weight_hbm, partial_ref,
    features_ref, w_in_ref, b_in_ref, out_weight_ref, pre_ref, done,
):
    pieces_in = done.shape[0] - 3
    deep = w_in_ref.shape[0] // pieces_in
    small = [
        pltpu.make_async_copy(features_hbm, features_ref, done.at[pieces_in]),
        pltpu.make_async_copy(b_in_hbm, b_in_ref, done.at[pieces_in + 1]),
        pltpu.make_async_copy(out_weight_hbm, out_weight_ref, done.at[pieces_in + 2]),
    ]
    parts = [
        pltpu.make_async_copy(
            w_in_hbm.at[k * deep : (k + 1) * deep], w_in_ref.at[k * deep : (k + 1) * deep], done.at[k]
        )
        for k in range(pieces_in)
    ]
    for copy in (small[0], *parts, *small[1:]):
        copy.start()
    small[0].wait()
    for k, copy in enumerate(parts):
        copy.wait()
        rows = slice(k * deep, (k + 1) * deep)
        part = jnp.dot(features_ref[:, rows], w_in_ref[rows, :], preferred_element_type=F32)
        pre_ref[...] = part if k == 0 else pre_ref[...] + part
    small[1].wait()
    hidden = jax.nn.gelu(pre_ref[...] + b_in_ref[...], approximate=True).astype(BF16)
    small[2].wait()
    partial_ref[...] = jnp.dot(hidden, out_weight_ref[...], preferred_element_type=F32)


def block_kernel(gains_ref, transition_ref, chain_ref, prefix_ref):
    grid = transition_ref.shape[0]
    chains = chain_ref.shape[0]
    flipped = transition_ref[...].T
    step = right(flipped)
    for j in range(chains):
        chain_ref[j] = flipped * (1.0 - gains_ref[SUB * j : SUB * j + 1, :])
    for t in range(1, SUB):
        for part in range(2):
            own = range(part * chains // 2, (part + 1) * chains // 2)
            moved = times(jnp.concatenate([chain_ref[j] for j in own], axis=0), step)
            for n, j in enumerate(own):
                row = SUB * j + t
                keep = 1.0 - gains_ref[row : row + 1, :]
                chain_ref[j] = moved[n * grid : (n + 1) * grid] * keep
    prefix_ref[0] = chain_ref[0]
    for j in range(1, chains):
        prefix_ref[j] = times(prefix_ref[j - 1], right(chain_ref[j]))


def response_kernel(
    one_ref, two_ref, three_ref, four_ref, offset_ref, gains_ref, transition_ref, chain_ref, prefix_ref,
    whole_ref, drive_ref, start_ref,
):
    chains, grid = chain_ref.shape[0], transition_ref.shape[0]
    step = right(transition_ref[...].T)
    measured = (one_ref[...] + two_ref[...]) + (three_ref[...] + four_ref[...])
    drive_ref[...] = gains_ref[...] * (measured + offset_ref[...])
    state = each(drive_ref, 0, chains)
    for t in range(1, SUB):
        keep = 1.0 - each(gains_ref, t, chains)
        state = times(state, step) * keep + each(drive_ref, t, chains)
    start_ref[...] = jnp.zeros_like(start_ref)
    carried = state[0:1]
    for j in range(1, chains):
        start_ref[j : j + 1, :] = carried
        carried = times(carried, right(chain_ref[j])) + state[j : j + 1]
    whole_ref[0:grid, :] = prefix_ref[chains - 1]
    whole_ref[grid:, :] = jnp.concatenate([carried, jnp.zeros((VEC - 1, grid), F32)], axis=0)


def after(earlier, later):
    grid = later.shape[1]
    added = jnp.concatenate([jnp.zeros((grid, grid), F32), later[grid:]], axis=0)
    return times(earlier, right(later[:grid])) + added


def ordered(held, own, other, upper):
    held[0] = own
    held[1] = other
    return after(held[upper], held[1 - upper])


def half_rows(whole_ref, half_ref, core):
    half = half_ref.shape[0] - VEC
    half_ref[0:half, :] = whole_ref[pl.ds(pl.multiple_of(core * half, half), half), :]
    half_ref[half:, :] = whole_ref[2 * half :, :]


def whole_kernel(level, own_ref, other_ref, whole_ref, half_ref, held):
    whole_ref[...] = ordered(held, own_ref[...], other_ref[...], bit(level))
    half_rows(whole_ref, half_ref, bit(0))


def join(mine_ref, theirs_ref, other_ref):
    half = mine_ref.shape[0] - VEC
    core = bit(0)
    other_ref[pl.ds(pl.multiple_of(core * half, half), half), :] = mine_ref[0:half, :]
    other_ref[pl.ds(pl.multiple_of((1 - core) * half, half), half), :] = theirs_ref[0:half, :]
    other_ref[2 * half :, :] = mine_ref[half:, :]


def halves_kernel(level, own_ref, mine_ref, theirs_ref, whole_ref, half_ref, other_ref, held):
    join(mine_ref, theirs_ref, other_ref)
    whole_ref[...] = ordered(held, own_ref[...], other_ref[...], bit(level))
    half_rows(whole_ref, half_ref, bit(0))


def end_kernel(level, own_ref, mine_ref, theirs_ref, end_ref, other_ref, held):
    grid = own_ref.shape[1]
    upper = bit(level)
    join(mine_ref, theirs_ref, other_ref)
    held[0] = own_ref[...]
    held[1] = other_ref[...]
    later = held.at[1 - upper]
    end_ref[...] = times(held[upper, grid:, :], right(later[:grid, :])) + later[grid:, :]


def starts_kernel(*refs):
    others, (prefix_ref, start_ref, starts_ref, shifts_ref, held) = refs[:4], refs[4:]
    chains, grid = prefix_ref.shape[0], prefix_ref.shape[2]
    top = others[3]
    row = lax.broadcasted_iota(jnp.int32, top.shape, 0)
    column = lax.broadcasted_iota(jnp.int32, top.shape, 1)
    held[...] = jnp.where(bit(3) > 0, top[...], jnp.where(row == column, 1.0, 0.0))
    for level in (2, 1, 0):
        @pl.when(bit(level) > 0)
        def _():
            held[...] = after(held[...], others[level][...])
    starts_ref[0] = held[:grid, :]
    rows = [held[grid : grid + 1, :]]
    for j in range(1, chains):
        moved = times(held[...], right(prefix_ref[j - 1]))
        starts_ref[j] = moved[:grid]
        rows.append(moved[grid : grid + 1] + start_ref[j : j + 1, :])
    shifts_ref[...] = jnp.concatenate([*rows, jnp.zeros((VEC - chains, grid), F32)], axis=0)


def advance(state, whole):
    grid = whole.shape[1]
    return times(state, right(whole[:grid])) + whole[grid : grid + 1]


def final_kernel(
    end_ref, group_ref, starts_ref, shifts_ref, drive_ref, gains_ref, smooth_ref, transition_ref,
    filtered_ref, weight_ref, value_ref, send_ref, found, scan_d, scan_v,
):
    chains = starts_ref.shape[0]
    frames, grid = drive_ref.shape
    part = lax.axis_index("y")
    last = lax.axis_index(TM) == lax.axis_size(TM) - 1
    step = right(transition_ref[...].T)
    state = jnp.where(bit(5) > 0, end_ref[...], 0.0)
    state = jnp.where(bit(4) > 0, advance(state, group_ref[...]), state)
    rows = [times(state, right(starts_ref[j]))[0:1] for j in range(chains)]
    now = jnp.concatenate(rows, axis=0) + shifts_ref[0:chains, :]
    for t in range(SUB):
        keep = 1.0 - each(gains_ref, t, chains)
        now = times(now, step) * keep + each(drive_ref, t, chains)
        for j in range(chains):
            found[SUB * j + t : SUB * j + t + 1, :] = now[j : j + 1]
    weight = smooth_ref[...]
    row = lax.broadcasted_iota(jnp.int32, (frames, grid), 0)
    weight = jnp.where((row == frames - 1) & last, 0.0, weight)
    value = found[...] - weight * times(found[...], step)
    d, v = weight[frames - 1 : frames], value[frames - 1 : frames]
    scan_d[frames - 1 : frames, :] = d
    scan_v[frames - 1 : frames, :] = v
    for t in range(frames - 2, -1, -1):
        v = weight[t : t + 1] * v + value[t : t + 1]
        d = weight[t : t + 1] * d
        scan_d[t : t + 1, :] = d
        scan_v[t : t + 1, :] = v
    share = filtered_ref.shape[0]
    mine = pl.ds(pl.multiple_of(part * share, share), share)
    filtered_ref[...] = found[mine, :]
    weight_ref[...] = scan_d[mine, :]
    value_ref[...] = scan_v[mine, :]
    send_ref[...] = jnp.broadcast_to(jnp.concatenate([d, v], axis=1), send_ref.shape)


def smooth_kernel(got_ref, weight_ref, value_ref, smoothed_ref):
    blocks = got_ref.shape[0]
    grid = weight_ref.shape[1]
    here = lax.axis_index(TM)
    row = lax.broadcasted_iota(jnp.int32, (blocks, grid), 0)
    d = jnp.where(row > here, got_ref[:, :grid], 1.0)
    v = jnp.where(row > here, got_ref[:, grid:], 0.0)
    later = jnp.zeros((1, grid), F32)
    for k in range(blocks - 1, -1, -1):
        later = d[k : k + 1] * later + v[k : k + 1]
    smoothed_ref[...] = weight_ref[...] * later + value_ref[...]


def shape(*dims):
    return jax.ShapeDtypeStruct(dims, F32)


V = pl.BlockSpec(memory_space=pltpu.VMEM)
ROOM = pltpu.CompilerParams(vmem_limit_bytes=12 << 20)


def call(kernel, ins, outs, out_shape, scratch=()):
    return pl.pallas_call(
        kernel, in_specs=ins, out_specs=outs, out_shape=out_shape,
        scratch_shapes=list(scratch), compiler_params=ROOM,
    )


def on_device(
    features, w_in, b_in, output_weight, final_offset_entries, transition, gains, smooth_gains
):
    frames, grid = gains.shape
    chains = frames // SUB
    rows = grid + VEC
    blocks = lax.axis_size(TM)
    parts = lax.axis_size("y")
    H = pl.BlockSpec(memory_space=pltpu.HBM)
    units = w_in.shape[1]
    partial = call(
        network_kernel, [H] * 4, V, shape(frames, grid),
        [
            pltpu.VMEM(features.shape, BF16), pltpu.VMEM(w_in.shape, BF16),
            pltpu.VMEM((1, units), F32), pltpu.VMEM(output_weight.shape, BF16),
            pltpu.VMEM((frames, units), F32), pltpu.SemaphoreType.DMA((8 + 3,)),
        ],
    )(*(pltpu.with_memory_space_constraint(a, pltpu.HBM) for a in (features, w_in, b_in[None], output_weight)))
    partials = [partial] + [
        lax.ppermute(partial, "y", [(k, (k + s) % parts) for k in range(parts)])
        for s in range(1, parts)
    ]

    chain, prefix = call(
        block_kernel, [V, V], [V, V],
        [shape(chains, grid, grid), shape(chains, grid, grid)],
    )(gains, transition)
    whole, drive, start = call(
        response_kernel, [V] * 9, [V] * 3,
        [shape(rows, grid), shape(frames, grid), shape(VEC, grid)],
    )(*partials, final_offset_entries[None], gains, transition, chain, prefix)

    big, small = shape(rows, grid), shape(grid // 2 + VEC, grid)
    held = [pltpu.VMEM((2, rows, grid), F32)]

    def moved(a, axis, to):
        return lax.ppermute(a, axis, [(k, to(k)) for k in range(lax.axis_size(axis))])

    ways = [
        ("c", lambda k: 1 - k), ("z", lambda k: k ^ 1), ("z", lambda k: k ^ 2),
        ("z", lambda k: 7 - k), ("x", lambda k: k ^ 1), ("x", lambda k: k ^ 2),
    ]
    others = [moved(whole, *ways[0])]
    whole, half = call(
        functools.partial(whole_kernel, 0), [V, V], [V, V], [big, small], held
    )(whole, others[0])
    for level in (1, 2, 3):
        mine = moved(half, *ways[level])
        theirs = moved(mine, *ways[0])
        whole, half, other = call(
            functools.partial(halves_kernel, level), [V] * 3, [V] * 3, [big, small, big], held
        )(whole, mine, theirs)
        others.append(other)
    mine = moved(half, *ways[4])
    theirs = moved(mine, *ways[0])
    end, group = call(
        functools.partial(end_kernel, 4), [V] * 3, [V, V], [shape(VEC, grid), big], held
    )(whole, mine, theirs)
    end = moved(end, *ways[5])
    starts, shifts = call(
        starts_kernel, [V] * 6, [V, V], [shape(chains, grid, grid), shape(VEC, grid)],
        [pltpu.VMEM((rows, grid), F32)],
    )(*others, prefix, start)

    share = frames // parts
    filtered, weight, value, send = call(
        final_kernel, [V] * 8, [V] * 4,
        [shape(share, grid)] * 3 + [shape(blocks, 2 * grid)],
        [pltpu.VMEM((frames, grid), F32)] * 3,
    )(end, group, starts, shifts, drive, gains, smooth_gains, transition)
    got = lax.all_to_all(send, TM, 0, 0, tiled=True)
    smoothed = call(smooth_kernel, [V, V, V], V, shape(share, grid))(
        got, weight, value
    )
    return filtered, smoothed


def solution(mesh):
    torus = Mesh(mesh.devices.reshape(4, 8, 2, mesh.shape["mp"]), ("x", "z", "c", "y"))
    return jax.shard_map(
        on_device,
        mesh=torus,
        in_specs=(
            P(TM, None), P(None, "y"), P("y"), P("y", None), P(), P(), P(TM, None), P(TM, None),
        ),
        out_specs=(P((*TM, "y"), None), P((*TM, "y"), None)),
        check_vma=False,
    )
```

```python
import functools

import jax
import jax.numpy as jnp
from jax import lax
from jax.experimental import pallas as pl
from jax.experimental.pallas import tpu as pltpu
from jax.sharding import Mesh
from jax.sharding import PartitionSpec as P

Z = ("q", "k")
TM = ("x", "q", "k", "c")
F32, BF16 = jnp.float32, jnp.bfloat16
SUB = 8
MERGED = 2
VEC = 8


def pieces(a):
    high = a.astype(BF16)
    return high, (a - high.astype(F32)).astype(BF16)


def right(b):
    return pieces(b)


def times(a, b):
    high, low = pieces(a)
    rows = a.shape[0]
    if rows > 16:
        both = jnp.concatenate([high, low, high], axis=1)
        return jnp.dot(both, jnp.concatenate([b[0], b[0], b[1]], axis=0), preferred_element_type=F32)
    top = jnp.dot(jnp.concatenate([high, low], axis=0), b[0], preferred_element_type=F32)
    return (top[:rows] + top[rows:]) + jnp.dot(high, b[1], preferred_element_type=F32)


def each(ref, t, chains):
    return jnp.concatenate([ref[SUB * j + t : SUB * j + t + 1, :] for j in range(chains)], axis=0)


def bit(level):
    if level == 0:
        return lax.axis_index("c")
    if level < 4:
        return (lax.axis_index(Z) >> (level - 1)) & 1
    return (lax.axis_index("x") >> (level - 4)) & 1


def network_kernel(
    features_hbm, w_in_hbm, b_in_hbm, out_weight_hbm, partial_ref,
    features_ref, w_in_ref, b_in_ref, out_weight_ref, pre_ref, done,
):
    pieces_in = done.shape[0] - 3
    deep = w_in_ref.shape[0] // pieces_in
    small = [
        pltpu.make_async_copy(features_hbm, features_ref, done.at[pieces_in]),
        pltpu.make_async_copy(b_in_hbm, b_in_ref, done.at[pieces_in + 1]),
        pltpu.make_async_copy(out_weight_hbm, out_weight_ref, done.at[pieces_in + 2]),
    ]
    parts = [
        pltpu.make_async_copy(
            w_in_hbm.at[k * deep : (k + 1) * deep], w_in_ref.at[k * deep : (k + 1) * deep], done.at[k]
        )
        for k in range(pieces_in)
    ]
    for copy in (small[0], *parts, *small[1:]):
        copy.start()
    small[0].wait()
    for k, copy in enumerate(parts):
        copy.wait()
        rows = slice(k * deep, (k + 1) * deep)
        part = jnp.dot(features_ref[:, rows], w_in_ref[rows, :], preferred_element_type=F32)
        pre_ref[...] = part if k == 0 else pre_ref[...] + part
    small[1].wait()
    hidden = jax.nn.gelu(pre_ref[...] + b_in_ref[...], approximate=True).astype(BF16)
    small[2].wait()
    partial_ref[...] = jnp.dot(hidden, out_weight_ref[...], preferred_element_type=F32)


def block_kernel(gains_ref, transition_ref, chain_ref, prefix_ref):
    grid = transition_ref.shape[0]
    chains = chain_ref.shape[0]
    flipped = transition_ref[...].T
    step = right(flipped)
    for j in range(chains):
        chain_ref[j] = flipped * (1.0 - gains_ref[SUB * j : SUB * j + 1, :])
    for t in range(1, SUB):
        for part in range(2):
            own = range(part * chains // 2, (part + 1) * chains // 2)
            moved = times(jnp.concatenate([chain_ref[j] for j in own], axis=0), step)
            for n, j in enumerate(own):
                row = SUB * j + t
                keep = 1.0 - gains_ref[row : row + 1, :]
                chain_ref[j] = moved[n * grid : (n + 1) * grid] * keep
    prefix_ref[0] = chain_ref[0]
    for j in range(1, chains):
        prefix_ref[j] = times(prefix_ref[j - 1], right(chain_ref[j]))


def response_kernel(
    one_ref, two_ref, three_ref, four_ref, offset_ref, gains_ref, transition_ref, chain_ref, prefix_ref,
    whole_ref, drive_ref, start_ref,
):
    chains, grid = chain_ref.shape[0], transition_ref.shape[0]
    step = right(transition_ref[...].T)
    measured = (one_ref[...] + two_ref[...]) + (three_ref[...] + four_ref[...])
    drive_ref[...] = gains_ref[...] * (measured + offset_ref[...])
    state = each(drive_ref, 0, chains)
    for t in range(1, SUB):
        keep = 1.0 - each(gains_ref, t, chains)
        state = times(state, step) * keep + each(drive_ref, t, chains)
    start_ref[...] = jnp.zeros_like(start_ref)
    carried = state[0:1]
    for j in range(1, chains):
        start_ref[j : j + 1, :] = carried
        carried = times(carried, right(chain_ref[j])) + state[j : j + 1]
    whole_ref[0:grid, :] = prefix_ref[chains - 1]
    whole_ref[grid:, :] = jnp.concatenate([carried, jnp.zeros((VEC - 1, grid), F32)], axis=0)


def after(earlier, later):
    grid = later.shape[1]
    added = jnp.concatenate([jnp.zeros((grid, grid), F32), later[grid:]], axis=0)
    return times(earlier, right(later[:grid])) + added


def closed(smooth_ref):
    frames, grid = smooth_ref.shape
    last = lax.axis_index(TM) == lax.axis_size(TM) - 1
    row = lax.broadcasted_iota(jnp.int32, (frames, grid), 0)
    return jnp.where((row == frames - 1) & last, 0.0, smooth_ref[...])


def summary_kernel(
    gains_ref, smooth_ref, transition_ref, drive_ref, prefix_ref, start_ref,
    sum_ref, walk, total, reach_ref,
):
    chains, grid = prefix_ref.shape[0], prefix_ref.shape[2]
    flipped = transition_ref[...].T
    step = right(flipped)
    weight = closed(smooth_ref)
    reach = jnp.ones((1, grid), F32)
    for t in range(weight.shape[0]):
        reach_ref[t : t + 1, :] = reach
        reach = reach * weight[t : t + 1]
    whole_reach = reach
    for j in range(chains):
        row = SUB * j
        walk[j, 0:grid, :] = flipped * (1.0 - gains_ref[row : row + 1, :])
        walk[j, grid:, :] = padded(drive_ref[row : row + 1, :])
    for t in range(SUB):
        for j in range(chains):
            row = SUB * j + t
            now = walk[j]
            moved = times(now, step)
            worth = (now - moved * weight[row : row + 1]) * reach_ref[row : row + 1, :]
            total[j] = worth if t == 0 else total[j] + worth
            if t < SUB - 1:
                keep = 1.0 - gains_ref[row + 1 : row + 2, :]
                walk[j, 0:grid, :] = moved[:grid] * keep
                walk[j, grid:, :] = moved[grid:] * keep + padded(drive_ref[row + 1 : row + 2, :])
    slope, rest = total[0, 0:grid, :], total[0, grid : grid + 1, :]
    for j in range(1, chains):
        entry = jnp.concatenate([prefix_ref[j - 1], padded(start_ref[j : j + 1, :])], axis=0)
        moved = times(entry, right(total[j, 0:grid, :]))
        slope = slope + moved[:grid]
        rest = rest + moved[grid : grid + 1] + total[j, grid : grid + 1, :]
    sum_ref[0:grid, :] = slope
    sum_ref[grid:, :] = jnp.concatenate(
        [rest, whole_reach, jnp.zeros((VEC - 2, grid), F32)], axis=0
    )


def merged_kernel(level, *refs):
    own_ref, other_ref, own_sum_ref, other_sum_ref, *before, sum_ref, later_ref = refs
    grid = own_ref.shape[1]
    upper = bit(level)

    def put(to_ref, slope, rest, reach):
        to_ref[0:grid, :] = slope
        to_ref[grid:, :] = jnp.concatenate([rest, reach, jnp.zeros((VEC - 2, grid), F32)], axis=0)

    def joined(first_ref, low_ref, high_ref):
        moved = times(first_ref[...], right(high_ref[0:grid, :]))
        slope, rest = moved[:grid], moved[grid : grid + 1] + high_ref[grid : grid + 1, :]
        low, high = low_ref[grid + 1 : grid + 2, :], high_ref[grid + 1 : grid + 2, :]
        put(
            sum_ref, low_ref[0:grid, :] + slope * low,
            low_ref[grid : grid + 1, :] + rest * low, low * high,
        )
        return slope, rest, high

    @pl.when(upper == 0)
    def _():
        slope, rest, high = joined(own_ref, own_sum_ref, other_sum_ref)
        if before:
            old = before[0]
            reach = old[grid + 1 : grid + 2, :]
            slope = old[0:grid, :] + slope * reach
            rest = old[grid : grid + 1, :] + rest * reach
            high = reach * high
        put(later_ref, slope, rest, high)

    @pl.when(upper > 0)
    def _():
        joined(other_ref, other_sum_ref, own_sum_ref)
        if before:
            old = before[0]
            moved = times(other_ref[...], right(old[0:grid, :]))
            put(
                later_ref, moved[:grid], moved[grid : grid + 1] + old[grid : grid + 1, :],
                old[grid + 1 : grid + 2, :],
            )
        else:
            nothing = jnp.zeros((grid, grid), F32)
            put(later_ref, nothing, nothing[0:1], nothing[0:1] + 1.0)


def padded(row):
    return jnp.concatenate([row, jnp.zeros((VEC - 1, row.shape[1]), F32)], axis=0)


def ordered(held, own, other, upper):
    held[0] = own
    held[1] = other
    return after(held[upper], held[1 - upper])


def half_rows(whole_ref, half_ref, core):
    half = half_ref.shape[0] - VEC
    half_ref[0:half, :] = whole_ref[pl.ds(pl.multiple_of(core * half, half), half), :]
    half_ref[half:, :] = whole_ref[2 * half :, :]


def whole_kernel(level, own_ref, other_ref, whole_ref, half_ref, held):
    whole_ref[...] = ordered(held, own_ref[...], other_ref[...], bit(level))
    half_rows(whole_ref, half_ref, bit(0))


def join(mine_ref, theirs_ref, other_ref):
    half = mine_ref.shape[0] - VEC
    core = bit(0)
    other_ref[pl.ds(pl.multiple_of(core * half, half), half), :] = mine_ref[0:half, :]
    other_ref[pl.ds(pl.multiple_of((1 - core) * half, half), half), :] = theirs_ref[0:half, :]
    other_ref[2 * half :, :] = mine_ref[half:, :]


def halves_kernel(level, own_ref, mine_ref, theirs_ref, whole_ref, half_ref, other_ref, held):
    join(mine_ref, theirs_ref, other_ref)
    whole_ref[...] = ordered(held, own_ref[...], other_ref[...], bit(level))
    half_rows(whole_ref, half_ref, bit(0))


def end_kernel(level, own_ref, mine_ref, theirs_ref, end_ref, other_ref, held):
    grid = own_ref.shape[1]
    upper = bit(level)
    join(mine_ref, theirs_ref, other_ref)
    held[0] = own_ref[...]
    held[1] = other_ref[...]
    later = held.at[1 - upper]
    end_ref[...] = times(held[upper, grid:, :], right(later[:grid, :])) + later[grid:, :]


def starts_kernel(*refs):
    others, (prefix_ref, start_ref, sum_ref, later_ref, starts_ref, shifts_ref, held) = refs[:4], refs[4:]
    chains, grid = prefix_ref.shape[0], prefix_ref.shape[2]
    top = others[3]
    row = lax.broadcasted_iota(jnp.int32, top.shape, 0)
    column = lax.broadcasted_iota(jnp.int32, top.shape, 1)
    held[...] = jnp.where(bit(3) > 0, top[...], jnp.where(row == column, 1.0, 0.0))
    tail = []
    for level in (2, 1, 0):
        if level == MERGED - 1:
            for k, part_ref in enumerate((sum_ref, later_ref)):
                moved = times(held[...], right(part_ref[0:grid, :]))
                starts_ref[chains + k] = moved[:grid]
                tail.append(moved[grid : grid + 1] + part_ref[grid : grid + 1, :])
                tail.append(part_ref[grid + 1 : grid + 2, :])

        @pl.when(bit(level) > 0)
        def _():
            held[...] = after(held[...], others[level][...])
    starts_ref[0] = held[:grid, :]
    rows = [held[grid : grid + 1, :]]
    for j in range(1, chains):
        moved = times(held[...], right(prefix_ref[j - 1]))
        starts_ref[j] = moved[:grid]
        rows.append(moved[grid : grid + 1] + start_ref[j : j + 1, :])
    shifts_ref[...] = jnp.concatenate([*rows, *tail], axis=0)


def send_kernel(end_ref, group_ref, starts_ref, shifts_ref, state_ref, send_ref):
    chains = starts_ref.shape[0] - 2
    state = jnp.where(bit(5) > 0, end_ref[...], 0.0)
    state = jnp.where(bit(4) > 0, advance(state, group_ref[...]), state)
    state_ref[...] = state
    v = times(state, right(starts_ref[chains]))[0:1] + shifts_ref[chains : chains + 1, :]
    d = shifts_ref[chains + 1 : chains + 2, :]
    send_ref[...] = jnp.broadcast_to(jnp.concatenate([d, v], axis=1)[None], send_ref.shape)


def advance(state, whole):
    grid = whole.shape[1]
    return times(state, right(whole[:grid])) + whole[grid : grid + 1]


def final_kernel(
    state_ref, starts_ref, shifts_ref, drive_ref, gains_ref, smooth_ref, transition_ref,
    filtered_ref, weight_ref, value_ref, found, scan_d, scan_v,
):
    chains = starts_ref.shape[0] - 2
    frames = drive_ref.shape[0]
    part = lax.axis_index("y")
    step = right(transition_ref[...].T)
    state = state_ref[...]
    rows = [times(state, right(starts_ref[j]))[0:1] for j in range(chains)]
    now = jnp.concatenate(rows, axis=0) + shifts_ref[0:chains, :]
    for t in range(SUB):
        keep = 1.0 - each(gains_ref, t, chains)
        now = times(now, step) * keep + each(drive_ref, t, chains)
        for j in range(chains):
            found[SUB * j + t : SUB * j + t + 1, :] = now[j : j + 1]
    weight = closed(smooth_ref)
    value = found[...] - weight * times(found[...], step)
    d, v = weight[frames - 1 : frames], value[frames - 1 : frames]
    scan_d[frames - 1 : frames, :] = d
    scan_v[frames - 1 : frames, :] = v
    for t in range(frames - 2, -1, -1):
        v = weight[t : t + 1] * v + value[t : t + 1]
        d = weight[t : t + 1] * d
        scan_d[t : t + 1, :] = d
        scan_v[t : t + 1, :] = v
    share = filtered_ref.shape[0]
    mine = pl.ds(pl.multiple_of(part * share, share), share)
    filtered_ref[...] = found[mine, :]
    later = times(state, right(starts_ref[chains + 1]))[0:1] + shifts_ref[chains + 2 : chains + 3, :]
    weight_ref[...] = scan_d[mine, :] * shifts_ref[chains + 3 : chains + 4, :]
    value_ref[...] = scan_d[mine, :] * later + scan_v[mine, :]


def smooth_kernel(got_ref, weight_ref, value_ref, smoothed_ref):
    blocks = got_ref.shape[0]
    grid = weight_ref.shape[1]
    here = lax.axis_index(TM) >> MERGED
    row = lax.broadcasted_iota(jnp.int32, (blocks, grid), 0)
    d = jnp.where(row > here, got_ref[:, :grid], 1.0)
    v = jnp.where(row > here, got_ref[:, grid:], 0.0)
    later = jnp.zeros((1, grid), F32)
    for k in range(blocks - 1, -1, -1):
        later = d[k : k + 1] * later + v[k : k + 1]
    smoothed_ref[...] = weight_ref[...] * later + value_ref[...]


def shape(*dims):
    return jax.ShapeDtypeStruct(dims, F32)


V = pl.BlockSpec(memory_space=pltpu.VMEM)
ROOM = pltpu.CompilerParams(vmem_limit_bytes=12 << 20)


def call(kernel, ins, outs, out_shape, scratch=()):
    return pl.pallas_call(
        kernel, in_specs=ins, out_specs=outs, out_shape=out_shape,
        scratch_shapes=list(scratch), compiler_params=ROOM,
    )


def on_device(
    features, w_in, b_in, output_weight, final_offset_entries, transition, gains, smooth_gains
):
    frames, grid = gains.shape
    chains = frames // SUB
    rows = grid + VEC
    among = TM[: len(TM) - MERGED]
    blocks = lax.axis_size(among)
    parts = lax.axis_size("y")
    H = pl.BlockSpec(memory_space=pltpu.HBM)
    units = w_in.shape[1]
    partial = call(
        network_kernel, [H] * 4, V, shape(frames, grid),
        [
            pltpu.VMEM(features.shape, BF16), pltpu.VMEM(w_in.shape, BF16),
            pltpu.VMEM((1, units), F32), pltpu.VMEM(output_weight.shape, BF16),
            pltpu.VMEM((frames, units), F32), pltpu.SemaphoreType.DMA((8 + 3,)),
        ],
    )(*(pltpu.with_memory_space_constraint(a, pltpu.HBM) for a in (features, w_in, b_in[None], output_weight)))
    partials = [partial] + [
        lax.ppermute(partial, "y", [(k, (k + s) % parts) for k in range(parts)])
        for s in range(1, parts)
    ]

    chain, prefix = call(
        block_kernel, [V, V], [V, V],
        [shape(chains, grid, grid), shape(chains, grid, grid)],
    )(gains, transition)
    whole, drive, start = call(
        response_kernel, [V] * 9, [V] * 3,
        [shape(rows, grid), shape(frames, grid), shape(VEC, grid)],
    )(*partials, final_offset_entries[None], gains, transition, chain, prefix)

    big, small = shape(rows, grid), shape(grid // 2 + VEC, grid)
    held = [pltpu.VMEM((2, rows, grid), F32)]

    def moved(a, axis, to):
        return lax.ppermute(a, axis, [(k, to(k)) for k in range(lax.axis_size(axis))])

    ways = [
        ("c", lambda k: 1 - k), (Z, lambda k: k ^ 1), (Z, lambda k: k ^ 2),
        (Z, lambda k: 7 - k), ("x", lambda k: k ^ 1), ("x", lambda k: k ^ 2),
    ]
    wholes = [whole]
    others = [moved(whole, *ways[0])]
    whole, half = call(
        functools.partial(whole_kernel, 0), [V, V], [V, V], [big, small], held
    )(whole, others[0])
    for level in (1, 2, 3):
        wholes.append(whole)
        mine = moved(half, *ways[level])
        if level == 2:
            drive, _ = lax.optimization_barrier((drive, half))
            total = call(
                summary_kernel, [V] * 6, V, big,
                [pltpu.VMEM((chains, rows, grid), F32)] * 2 + [pltpu.VMEM((frames, grid), F32)],
            )(gains, smooth_gains, transition, drive, prefix, start)
            mine, total = lax.optimization_barrier((mine, total))
        if level == 3:
            total, later = call(
                functools.partial(merged_kernel, 0), [V] * 4, [V, V], [big, big]
            )(wholes[0], others[0], total, moved(total, *ways[0]))
            mine, total = lax.optimization_barrier((mine, total))
        theirs = moved(mine, *ways[0])
        whole, half, other = call(
            functools.partial(halves_kernel, level), [V] * 3, [V] * 3, [big, small, big], held
        )(whole, mine, theirs)
        others.append(other)
    mine = moved(half, *ways[4])
    if MERGED > 1:
        total, _ = lax.optimization_barrier((total, half))
        total, later = call(
            functools.partial(merged_kernel, 1), [V] * 5, [V, V], [big, big]
        )(wholes[1], others[1], total, moved(total, *ways[1]), later)
    theirs = moved(mine, *ways[0])
    end, group = call(
        functools.partial(end_kernel, 4), [V] * 3, [V, V], [shape(VEC, grid), big], held
    )(whole, mine, theirs)
    end = moved(end, *ways[5])
    starts, shifts = call(
        starts_kernel, [V] * 8, [V, V], [shape(chains + 2, grid, grid), shape(VEC, grid)],
        [pltpu.VMEM((rows, grid), F32)],
    )(*others, prefix, start, total, later)

    share = frames // parts
    state, send = call(
        send_kernel, [V] * 4, [V, V], [shape(VEC, grid), shape(blocks, 1, 2 * grid)]
    )(end, group, starts, shifts)
    got = lax.all_to_all(send, among, 0, 0, tiled=True)[:, 0]
    filtered, weight, value = call(
        final_kernel, [V] * 7, [V] * 3, [shape(share, grid)] * 3,
        [pltpu.VMEM((frames, grid), F32)] * 3,
    )(state, starts, shifts, drive, gains, smooth_gains, transition)
    smoothed = call(smooth_kernel, [V, V, V], V, shape(share, grid))(
        got, weight, value
    )
    return filtered, smoothed


def solution(mesh):
    torus = Mesh(mesh.devices.reshape(4, 4, 2, 2, mesh.shape["mp"]), ("x", "q", "k", "c", "y"))
    return jax.shard_map(
        on_device,
        mesh=torus,
        in_specs=(
            P(TM, None), P(None, "y"), P("y"), P("y", None), P(), P(), P(TM, None), P(TM, None),
        ),
        out_specs=(P((*TM, "y"), None), P((*TM, "y"), None)),
        check_vma=False,
    )
```

```python
import functools

import jax
import jax.numpy as jnp
from jax import lax
from jax.experimental import pallas as pl
from jax.experimental.pallas import tpu as pltpu
from jax.sharding import Mesh
from jax.sharding import PartitionSpec as P

Z = ("q", "k")
TM = ("x", "q", "k", "c")
F32, BF16 = jnp.float32, jnp.bfloat16
SUB = 8
MERGED = 2
VEC = 8


def pieces(a):
    high = a.astype(BF16)
    return high, (a - high.astype(F32)).astype(BF16)


def right(b):
    return pieces(b)


def times(a, b):
    high, low = pieces(a)
    rows = a.shape[0]
    if rows > 16:
        both = jnp.concatenate([high, low, high], axis=1)
        return jnp.dot(both, jnp.concatenate([b[0], b[0], b[1]], axis=0), preferred_element_type=F32)
    top = jnp.dot(jnp.concatenate([high, low], axis=0), b[0], preferred_element_type=F32)
    return (top[:rows] + top[rows:]) + jnp.dot(high, b[1], preferred_element_type=F32)


def each(ref, t, chains):
    return jnp.concatenate([ref[SUB * j + t : SUB * j + t + 1, :] for j in range(chains)], axis=0)


def bit(level):
    if level == 0:
        return lax.axis_index("c")
    if level < 4:
        return (lax.axis_index(Z) >> (level - 1)) & 1
    return (lax.axis_index("x") >> (level - 4)) & 1


def network_kernel(
    features_hbm, w_in_hbm, b_in_hbm, out_weight_hbm, partial_ref,
    features_ref, w_in_ref, b_in_ref, out_weight_ref, pre_ref, done,
):
    pieces_in = done.shape[0] - 3
    deep = w_in_ref.shape[0] // pieces_in
    small = [
        pltpu.make_async_copy(features_hbm, features_ref, done.at[pieces_in]),
        pltpu.make_async_copy(b_in_hbm, b_in_ref, done.at[pieces_in + 1]),
        pltpu.make_async_copy(out_weight_hbm, out_weight_ref, done.at[pieces_in + 2]),
    ]
    parts = [
        pltpu.make_async_copy(
            w_in_hbm.at[k * deep : (k + 1) * deep], w_in_ref.at[k * deep : (k + 1) * deep], done.at[k]
        )
        for k in range(pieces_in)
    ]
    for copy in (small[0], *parts, *small[1:]):
        copy.start()
    small[0].wait()
    for k, copy in enumerate(parts):
        copy.wait()
        rows = slice(k * deep, (k + 1) * deep)
        part = jnp.dot(features_ref[:, rows], w_in_ref[rows, :], preferred_element_type=F32)
        pre_ref[...] = part if k == 0 else pre_ref[...] + part
    small[1].wait()
    hidden = jax.nn.gelu(pre_ref[...] + b_in_ref[...], approximate=True).astype(BF16)
    small[2].wait()
    partial_ref[...] = jnp.dot(hidden, out_weight_ref[...], preferred_element_type=F32)


def block_kernel(gains_ref, transition_ref, chain_ref, prefix_ref):
    grid = transition_ref.shape[0]
    chains = chain_ref.shape[0]
    flipped = transition_ref[...].T
    step = right(flipped)
    for j in range(chains):
        chain_ref[j] = flipped * (1.0 - gains_ref[SUB * j : SUB * j + 1, :])
    for t in range(1, SUB):
        for part in range(2):
            own = range(part * chains // 2, (part + 1) * chains // 2)
            moved = times(jnp.concatenate([chain_ref[j] for j in own], axis=0), step)
            for n, j in enumerate(own):
                row = SUB * j + t
                keep = 1.0 - gains_ref[row : row + 1, :]
                chain_ref[j] = moved[n * grid : (n + 1) * grid] * keep
    prefix_ref[0] = chain_ref[0]
    for j in range(1, chains):
        prefix_ref[j] = times(prefix_ref[j - 1], right(chain_ref[j]))


def response_kernel(
    one_ref, two_ref, three_ref, four_ref, offset_ref, gains_ref, transition_ref, chain_ref, prefix_ref,
    whole_ref, drive_ref, start_ref,
):
    chains, grid = chain_ref.shape[0], transition_ref.shape[0]
    step = right(transition_ref[...].T)
    measured = (one_ref[...] + two_ref[...]) + (three_ref[...] + four_ref[...])
    drive_ref[...] = gains_ref[...] * (measured + offset_ref[...])
    state = each(drive_ref, 0, chains)
    for t in range(1, SUB):
        keep = 1.0 - each(gains_ref, t, chains)
        state = times(state, step) * keep + each(drive_ref, t, chains)
    start_ref[...] = jnp.zeros_like(start_ref)
    carried = state[0:1]
    for j in range(1, chains):
        start_ref[j : j + 1, :] = carried
        carried = times(carried, right(chain_ref[j])) + state[j : j + 1]
    whole_ref[0:grid, :] = prefix_ref[chains - 1]
    whole_ref[grid:, :] = jnp.concatenate([carried, jnp.zeros((VEC - 1, grid), F32)], axis=0)


def after(earlier, later):
    grid = later.shape[1]
    added = jnp.concatenate([jnp.zeros((grid, grid), F32), later[grid:]], axis=0)
    return times(earlier, right(later[:grid])) + added


def closed(smooth_ref):
    frames, grid = smooth_ref.shape
    last = lax.axis_index(TM) == lax.axis_size(TM) - 1
    row = lax.broadcasted_iota(jnp.int32, (frames, grid), 0)
    return jnp.where((row == frames - 1) & last, 0.0, smooth_ref[...])


def summary_kernel(
    gains_ref, smooth_ref, transition_ref, drive_ref, prefix_ref, start_ref,
    sum_ref, walk, total, reach_ref,
):
    chains, grid = prefix_ref.shape[0], prefix_ref.shape[2]
    flipped = transition_ref[...].T
    step = right(flipped)
    weight = closed(smooth_ref)
    reach = jnp.ones((1, grid), F32)
    for t in range(weight.shape[0]):
        reach_ref[t : t + 1, :] = reach
        reach = reach * weight[t : t + 1]
    whole_reach = reach
    for j in range(chains):
        row = SUB * j
        walk[j, 0:grid, :] = flipped * (1.0 - gains_ref[row : row + 1, :])
        walk[j, grid:, :] = padded(drive_ref[row : row + 1, :])
    for t in range(SUB):
        for j in range(chains):
            row = SUB * j + t
            now = walk[j]
            moved = times(now, step)
            worth = (now - moved * weight[row : row + 1]) * reach_ref[row : row + 1, :]
            total[j] = worth if t == 0 else total[j] + worth
            if t < SUB - 1:
                keep = 1.0 - gains_ref[row + 1 : row + 2, :]
                walk[j, 0:grid, :] = moved[:grid] * keep
                walk[j, grid:, :] = moved[grid:] * keep + padded(drive_ref[row + 1 : row + 2, :])
    slope, rest = total[0, 0:grid, :], total[0, grid : grid + 1, :]
    for j in range(1, chains):
        entry = jnp.concatenate([prefix_ref[j - 1], padded(start_ref[j : j + 1, :])], axis=0)
        moved = times(entry, right(total[j, 0:grid, :]))
        slope = slope + moved[:grid]
        rest = rest + moved[grid : grid + 1] + total[j, grid : grid + 1, :]
    sum_ref[0:grid, :] = slope
    sum_ref[grid:, :] = jnp.concatenate(
        [rest, whole_reach, jnp.zeros((VEC - 2, grid), F32)], axis=0
    )


def merged_kernel(level, *refs):
    own_ref, other_ref, own_sum_ref, other_sum_ref, *before, sum_ref, later_ref = refs
    grid = own_ref.shape[1]
    upper = bit(level)

    def put(to_ref, slope, rest, reach):
        to_ref[0:grid, :] = slope
        to_ref[grid:, :] = jnp.concatenate([rest, reach, jnp.zeros((VEC - 2, grid), F32)], axis=0)

    def joined(first_ref, low_ref, high_ref):
        moved = times(first_ref[...], right(high_ref[0:grid, :]))
        slope, rest = moved[:grid], moved[grid : grid + 1] + high_ref[grid : grid + 1, :]
        low, high = low_ref[grid + 1 : grid + 2, :], high_ref[grid + 1 : grid + 2, :]
        put(
            sum_ref, low_ref[0:grid, :] + slope * low,
            low_ref[grid : grid + 1, :] + rest * low, low * high,
        )
        return slope, rest, high

    @pl.when(upper == 0)
    def _():
        slope, rest, high = joined(own_ref, own_sum_ref, other_sum_ref)
        if before:
            old = before[0]
            reach = old[grid + 1 : grid + 2, :]
            slope = old[0:grid, :] + slope * reach
            rest = old[grid : grid + 1, :] + rest * reach
            high = reach * high
        put(later_ref, slope, rest, high)

    @pl.when(upper > 0)
    def _():
        joined(other_ref, other_sum_ref, own_sum_ref)
        if before:
            old = before[0]
            moved = times(other_ref[...], right(old[0:grid, :]))
            put(
                later_ref, moved[:grid], moved[grid : grid + 1] + old[grid : grid + 1, :],
                old[grid + 1 : grid + 2, :],
            )
        else:
            nothing = jnp.zeros((grid, grid), F32)
            put(later_ref, nothing, nothing[0:1], nothing[0:1] + 1.0)


def padded(row):
    return jnp.concatenate([row, jnp.zeros((VEC - 1, row.shape[1]), F32)], axis=0)


def ordered(held, own, other, upper):
    held[0] = own
    held[1] = other
    return after(held[upper], held[1 - upper])


def half_rows(whole_ref, half_ref, core):
    half = half_ref.shape[0] - VEC
    half_ref[0:half, :] = whole_ref[pl.ds(pl.multiple_of(core * half, half), half), :]
    half_ref[half:, :] = whole_ref[2 * half :, :]


def whole_kernel(level, own_ref, other_ref, whole_ref, half_ref, held):
    whole_ref[...] = ordered(held, own_ref[...], other_ref[...], bit(level))
    half_rows(whole_ref, half_ref, bit(0))


def join(mine_ref, theirs_ref, other_ref):
    half = mine_ref.shape[0] - VEC
    core = bit(0)
    other_ref[pl.ds(pl.multiple_of(core * half, half), half), :] = mine_ref[0:half, :]
    other_ref[pl.ds(pl.multiple_of((1 - core) * half, half), half), :] = theirs_ref[0:half, :]
    other_ref[2 * half :, :] = mine_ref[half:, :]


def halves_kernel(level, own_ref, mine_ref, theirs_ref, whole_ref, half_ref, other_ref, held):
    join(mine_ref, theirs_ref, other_ref)
    whole_ref[...] = ordered(held, own_ref[...], other_ref[...], bit(level))
    half_rows(whole_ref, half_ref, bit(0))


def end_kernel(level, own_ref, mine_ref, theirs_ref, end_ref, other_ref, held):
    grid = own_ref.shape[1]
    upper = bit(level)
    join(mine_ref, theirs_ref, other_ref)
    held[0] = own_ref[...]
    held[1] = other_ref[...]
    later = held.at[1 - upper]
    end_ref[...] = times(held[upper, grid:, :], right(later[:grid, :])) + later[grid:, :]


def starts_kernel(*refs):
    others, (prefix_ref, start_ref, sum_ref, later_ref, starts_ref, shifts_ref, held) = refs[:4], refs[4:]
    chains, grid = prefix_ref.shape[0], prefix_ref.shape[2]
    top = others[3]
    row = lax.broadcasted_iota(jnp.int32, top.shape, 0)
    column = lax.broadcasted_iota(jnp.int32, top.shape, 1)
    held[...] = jnp.where(bit(3) > 0, top[...], jnp.where(row == column, 1.0, 0.0))
    tail = []
    for level in (2, 1, 0):
        if level == MERGED - 1:
            for k, part_ref in enumerate((sum_ref, later_ref)):
                moved = times(held[...], right(part_ref[0:grid, :]))
                starts_ref[chains + k] = moved[:grid]
                tail.append(moved[grid : grid + 1] + part_ref[grid : grid + 1, :])
                tail.append(part_ref[grid + 1 : grid + 2, :])

        @pl.when(bit(level) > 0)
        def _():
            held[...] = after(held[...], others[level][...])
    starts_ref[0] = held[:grid, :]
    rows = [held[grid : grid + 1, :]]
    for j in range(1, chains):
        moved = times(held[...], right(prefix_ref[j - 1]))
        starts_ref[j] = moved[:grid]
        rows.append(moved[grid : grid + 1] + start_ref[j : j + 1, :])
    shifts_ref[...] = jnp.concatenate([*rows, *tail], axis=0)


def send_kernel(end_ref, group_ref, starts_ref, shifts_ref, state_ref, send_ref):
    chains = starts_ref.shape[0] - 2
    state = jnp.where(bit(5) > 0, end_ref[...], 0.0)
    state = jnp.where(bit(4) > 0, advance(state, group_ref[...]), state)
    state_ref[...] = state
    v = times(state, right(starts_ref[chains]))[0:1] + shifts_ref[chains : chains + 1, :]
    d = shifts_ref[chains + 1 : chains + 2, :]
    send_ref[...] = jnp.broadcast_to(jnp.concatenate([d, v], axis=1)[None], send_ref.shape)


def advance(state, whole):
    grid = whole.shape[1]
    return times(state, right(whole[:grid])) + whole[grid : grid + 1]


def final_kernel(
    state_ref, starts_ref, shifts_ref, drive_ref, gains_ref, smooth_ref, transition_ref,
    filtered_ref, weight_ref, value_ref, found, scan_d, scan_v,
):
    chains = starts_ref.shape[0] - 2
    frames = drive_ref.shape[0]
    part = lax.axis_index("y")
    step = right(transition_ref[...].T)
    state = state_ref[...]
    rows = [times(state, right(starts_ref[j]))[0:1] for j in range(chains)]
    now = jnp.concatenate(rows, axis=0) + shifts_ref[0:chains, :]
    for t in range(SUB):
        keep = 1.0 - each(gains_ref, t, chains)
        now = times(now, step) * keep + each(drive_ref, t, chains)
        for j in range(chains):
            found[SUB * j + t : SUB * j + t + 1, :] = now[j : j + 1]
    weight = closed(smooth_ref)
    value = found[...] - weight * times(found[...], step)
    d, v = weight[frames - 1 : frames], value[frames - 1 : frames]
    scan_d[frames - 1 : frames, :] = d
    scan_v[frames - 1 : frames, :] = v
    for t in range(frames - 2, -1, -1):
        v = weight[t : t + 1] * v + value[t : t + 1]
        d = weight[t : t + 1] * d
        scan_d[t : t + 1, :] = d
        scan_v[t : t + 1, :] = v
    share = filtered_ref.shape[0]
    mine = pl.ds(pl.multiple_of(part * share, share), share)
    filtered_ref[...] = found[mine, :]
    later = times(state, right(starts_ref[chains + 1]))[0:1] + shifts_ref[chains + 2 : chains + 3, :]
    weight_ref[...] = scan_d[mine, :] * shifts_ref[chains + 3 : chains + 4, :]
    value_ref[...] = scan_d[mine, :] * later + scan_v[mine, :]


def smooth_kernel(got_ref, weight_ref, value_ref, smoothed_ref):
    blocks = got_ref.shape[0]
    grid = weight_ref.shape[1]
    here = lax.axis_index(TM) >> MERGED
    row = lax.broadcasted_iota(jnp.int32, (blocks, grid), 0)
    d = jnp.where(row > here, got_ref[:, :grid], 1.0)
    v = jnp.where(row > here, got_ref[:, grid:], 0.0)
    later = jnp.zeros((1, grid), F32)
    for k in range(blocks - 1, -1, -1):
        later = d[k : k + 1] * later + v[k : k + 1]
    smoothed_ref[...] = weight_ref[...] * later + value_ref[...]


def shape(*dims):
    return jax.ShapeDtypeStruct(dims, F32)


V = pl.BlockSpec(memory_space=pltpu.VMEM)
ROOM = pltpu.CompilerParams(vmem_limit_bytes=12 << 20)


def call(kernel, ins, outs, out_shape, scratch=()):
    return pl.pallas_call(
        kernel, in_specs=ins, out_specs=outs, out_shape=out_shape,
        scratch_shapes=list(scratch), compiler_params=ROOM,
    )


def on_device(
    features, w_in, b_in, output_weight, final_offset_entries, transition, gains, smooth_gains
):
    frames, grid = gains.shape
    chains = frames // SUB
    rows = grid + VEC
    among = TM[: len(TM) - MERGED]
    blocks = lax.axis_size(among)
    parts = lax.axis_size("y")
    H = pl.BlockSpec(memory_space=pltpu.HBM)
    units = w_in.shape[1]
    partial = call(
        network_kernel, [H] * 4, V, shape(frames, grid),
        [
            pltpu.VMEM(features.shape, BF16), pltpu.VMEM(w_in.shape, BF16),
            pltpu.VMEM((1, units), F32), pltpu.VMEM(output_weight.shape, BF16),
            pltpu.VMEM((frames, units), F32), pltpu.SemaphoreType.DMA((8 + 3,)),
        ],
    )(*(pltpu.with_memory_space_constraint(a, pltpu.HBM) for a in (features, w_in, b_in[None], output_weight)))
    partials = [partial] + [
        lax.ppermute(partial, "y", [(k, (k + s) % parts) for k in range(parts)])
        for s in range(1, parts)
    ]

    chain, prefix = call(
        block_kernel, [V, V], [V, V],
        [shape(chains, grid, grid), shape(chains, grid, grid)],
    )(gains, transition)
    whole, drive, start = call(
        response_kernel, [V] * 9, [V] * 3,
        [shape(rows, grid), shape(frames, grid), shape(VEC, grid)],
    )(*partials, final_offset_entries[None], gains, transition, chain, prefix)

    big, small = shape(rows, grid), shape(grid // 2 + VEC, grid)
    held = [pltpu.VMEM((2, rows, grid), F32)]

    def moved(a, axis, to):
        return lax.ppermute(a, axis, [(k, to(k)) for k in range(lax.axis_size(axis))])

    ways = [
        ("c", lambda k: 1 - k), (Z, lambda k: k ^ 1), (Z, lambda k: k ^ 3),
        (Z, lambda k: 7 - k), ("x", lambda k: k ^ 1), ("x", lambda k: 3 - k),
    ]
    wholes = [whole]
    others = [moved(whole, *ways[0])]
    whole, half = call(
        functools.partial(whole_kernel, 0), [V, V], [V, V], [big, small], held
    )(whole, others[0])
    for level in (1, 2, 3):
        wholes.append(whole)
        mine = moved(half, *ways[level])
        if level == 2:
            drive, _ = lax.optimization_barrier((drive, half))
            total = call(
                summary_kernel, [V] * 6, V, big,
                [pltpu.VMEM((chains, rows, grid), F32)] * 2 + [pltpu.VMEM((frames, grid), F32)],
            )(gains, smooth_gains, transition, drive, prefix, start)
            mine, total = lax.optimization_barrier((mine, total))
        if level == 3:
            total, later = call(
                functools.partial(merged_kernel, 0), [V] * 4, [V, V], [big, big]
            )(wholes[0], others[0], total, moved(total, *ways[0]))
            mine, total = lax.optimization_barrier((mine, total))
        theirs = moved(mine, *ways[0])
        whole, half, other = call(
            functools.partial(halves_kernel, level), [V] * 3, [V] * 3, [big, small, big], held
        )(whole, mine, theirs)
        others.append(other)
    mine = moved(half, *ways[4])
    if MERGED > 1:
        total, _ = lax.optimization_barrier((total, half))
        total, later = call(
            functools.partial(merged_kernel, 1), [V] * 5, [V, V], [big, big]
        )(wholes[1], others[1], total, moved(total, *ways[1]), later)
    theirs = moved(mine, *ways[0])
    end, group = call(
        functools.partial(end_kernel, 4), [V] * 3, [V, V], [shape(VEC, grid), big], held
    )(whole, mine, theirs)
    end = moved(end, *ways[5])
    starts, shifts = call(
        starts_kernel, [V] * 8, [V, V], [shape(chains + 2, grid, grid), shape(VEC, grid)],
        [pltpu.VMEM((rows, grid), F32)],
    )(*others, prefix, start, total, later)

    share = frames // parts
    state, send = call(
        send_kernel, [V] * 4, [V, V], [shape(VEC, grid), shape(blocks, 1, 2 * grid)]
    )(end, group, starts, shifts)
    got = lax.all_to_all(send, among, 0, 0, tiled=True)[:, 0]
    filtered, weight, value = call(
        final_kernel, [V] * 7, [V] * 3, [shape(share, grid)] * 3,
        [pltpu.VMEM((frames, grid), F32)] * 3,
    )(state, starts, shifts, drive, gains, smooth_gains, transition)
    smoothed = call(smooth_kernel, [V, V, V], V, shape(share, grid))(
        got, weight, value
    )
    return filtered, smoothed


def solution(mesh):
    torus = Mesh(mesh.devices.reshape(4, 4, 2, 2, mesh.shape["mp"]), ("x", "q", "k", "c", "y"))
    return jax.shard_map(
        on_device,
        mesh=torus,
        in_specs=(
            P(TM, None), P(None, "y"), P("y"), P("y", None), P(), P(), P(TM, None), P(TM, None),
        ),
        out_specs=(P((*TM, "y"), None), P((*TM, "y"), None)),
        check_vma=False,
    )
```

```python
import functools

import jax
import jax.numpy as jnp
from jax import lax
from jax.experimental import pallas as pl
from jax.experimental.pallas import tpu as pltpu
from jax.sharding import Mesh
from jax.sharding import PartitionSpec as P

Z = ("q", "k")
TM = ("x", "q", "k", "c")
F32, BF16 = jnp.float32, jnp.bfloat16
SUB = 8
EARLY = 4
MERGED = 2
VEC = 8


def pieces(a):
    high = a.astype(BF16)
    return high, (a - high.astype(F32)).astype(BF16)


def right(b):
    return pieces(b)


def times(a, b):
    high, low = pieces(a)
    rows = a.shape[0]
    if rows > 16:
        both = jnp.concatenate([high, low, high], axis=1)
        return jnp.dot(both, jnp.concatenate([b[0], b[0], b[1]], axis=0), preferred_element_type=F32)
    top = jnp.dot(jnp.concatenate([high, low], axis=0), b[0], preferred_element_type=F32)
    return (top[:rows] + top[rows:]) + jnp.dot(high, b[1], preferred_element_type=F32)


def each(ref, t, chains):
    return jnp.concatenate([ref[SUB * j + t : SUB * j + t + 1, :] for j in range(chains)], axis=0)


def bit(level):
    if level == 0:
        return lax.axis_index("c")
    if level < 4:
        return (lax.axis_index(Z) >> (level - 1)) & 1
    return (lax.axis_index("x") >> (level - 4)) & 1


def network_kernel(
    features_hbm, w_in_hbm, b_in_hbm, out_weight_hbm, gains_hbm, transition_hbm,
    partial_ref, chain_ref,
    features_ref, w_in_ref, b_in_ref, out_weight_ref, gains_ref, transition_ref, pre_ref, done,
):
    pieces_in = done.shape[0] - 5
    deep = w_in_ref.shape[0] // pieces_in
    small = [
        pltpu.make_async_copy(features_hbm, features_ref, done.at[pieces_in]),
        pltpu.make_async_copy(b_in_hbm, b_in_ref, done.at[pieces_in + 1]),
        pltpu.make_async_copy(out_weight_hbm, out_weight_ref, done.at[pieces_in + 2]),
        pltpu.make_async_copy(gains_hbm, gains_ref, done.at[pieces_in + 3]),
        pltpu.make_async_copy(transition_hbm, transition_ref, done.at[pieces_in + 4]),
    ]
    parts = [
        pltpu.make_async_copy(
            w_in_hbm.at[k * deep : (k + 1) * deep], w_in_ref.at[k * deep : (k + 1) * deep], done.at[k]
        )
        for k in range(pieces_in)
    ]
    for copy in (small[4], small[3], small[0], *parts, *small[1:3]):
        copy.start()
    small[4].wait()
    small[3].wait()
    flipped = transition_ref[...].T
    for j in range(chain_ref.shape[0]):
        chain_ref[j] = flipped * (1.0 - gains_ref[SUB * j : SUB * j + 1, :])
    walked(chain_ref, gains_ref, right(flipped), 1, EARLY)
    small[0].wait()
    for k, copy in enumerate(parts):
        copy.wait()
        rows = slice(k * deep, (k + 1) * deep)
        part = jnp.dot(features_ref[:, rows], w_in_ref[rows, :], preferred_element_type=F32)
        pre_ref[...] = part if k == 0 else pre_ref[...] + part
    small[1].wait()
    hidden = jax.nn.gelu(pre_ref[...] + b_in_ref[...], approximate=True).astype(BF16)
    small[2].wait()
    partial_ref[...] = jnp.dot(hidden, out_weight_ref[...], preferred_element_type=F32)


def walked(chain_ref, gains_ref, step, first, last):
    chains, grid = chain_ref.shape[0], chain_ref.shape[1]
    for t in range(first, last):
        for part in range(2):
            own = range(part * chains // 2, (part + 1) * chains // 2)
            moved = times(jnp.concatenate([chain_ref[j] for j in own], axis=0), step)
            for n, j in enumerate(own):
                row = SUB * j + t
                keep = 1.0 - gains_ref[row : row + 1, :]
                chain_ref[j] = moved[n * grid : (n + 1) * grid] * keep


def block_kernel(gains_ref, transition_ref, early_ref, whole_ref, chain_ref, prefix_ref):
    chains = chain_ref.shape[0]
    chain_ref[...] = early_ref[...]
    walked(chain_ref, gains_ref, right(transition_ref[...].T), EARLY, SUB)
    prefix_ref[0] = chain_ref[0]
    for j in range(1, chains):
        prefix_ref[j] = times(prefix_ref[j - 1], right(chain_ref[j]))
    whole_ref[...] = prefix_ref[chains - 1]


def response_kernel(
    one_ref, two_ref, three_ref, four_ref, offset_ref, gains_ref, transition_ref, chain_ref,
    ended_ref, drive_ref, start_ref,
):
    chains, grid = chain_ref.shape[0], transition_ref.shape[0]
    step = right(transition_ref[...].T)
    measured = (one_ref[...] + two_ref[...]) + (three_ref[...] + four_ref[...])
    drive_ref[...] = gains_ref[...] * (measured + offset_ref[...])
    state = each(drive_ref, 0, chains)
    for t in range(1, SUB):
        keep = 1.0 - each(gains_ref, t, chains)
        state = times(state, step) * keep + each(drive_ref, t, chains)
    start_ref[...] = jnp.zeros_like(start_ref)
    carried = state[0:1]
    for j in range(1, chains):
        start_ref[j : j + 1, :] = carried
        carried = times(carried, right(chain_ref[j])) + state[j : j + 1]
    ended_ref[...] = padded(carried)


def after(earlier, later):
    grid = later.shape[1]
    added = jnp.concatenate([jnp.zeros((grid, grid), F32), later[grid:]], axis=0)
    return times(earlier, right(later[:grid])) + added


def closed(smooth_ref):
    frames, grid = smooth_ref.shape
    last = lax.axis_index(TM) == lax.axis_size(TM) - 1
    row = lax.broadcasted_iota(jnp.int32, (frames, grid), 0)
    return jnp.where((row == frames - 1) & last, 0.0, smooth_ref[...])


def summary_kernel(
    gains_ref, smooth_ref, transition_ref, drive_ref, prefix_ref, start_ref,
    sum_ref, walk, total, reach_ref,
):
    chains, grid = prefix_ref.shape[0], prefix_ref.shape[2]
    flipped = transition_ref[...].T
    step = right(flipped)
    weight = closed(smooth_ref)
    reach = jnp.ones((1, grid), F32)
    for t in range(weight.shape[0]):
        reach_ref[t : t + 1, :] = reach
        reach = reach * weight[t : t + 1]
    whole_reach = reach
    for j in range(chains):
        row = SUB * j
        walk[j, 0:grid, :] = flipped * (1.0 - gains_ref[row : row + 1, :])
        walk[j, grid:, :] = padded(drive_ref[row : row + 1, :])
    for t in range(SUB):
        for j in range(chains):
            row = SUB * j + t
            now = walk[j]
            moved = times(now, step)
            worth = (now - moved * weight[row : row + 1]) * reach_ref[row : row + 1, :]
            total[j] = worth if t == 0 else total[j] + worth
            if t < SUB - 1:
                keep = 1.0 - gains_ref[row + 1 : row + 2, :]
                walk[j, 0:grid, :] = moved[:grid] * keep
                walk[j, grid:, :] = moved[grid:] * keep + padded(drive_ref[row + 1 : row + 2, :])
    slope, rest = total[0, 0:grid, :], total[0, grid : grid + 1, :]
    for j in range(1, chains):
        entry = jnp.concatenate([prefix_ref[j - 1], padded(start_ref[j : j + 1, :])], axis=0)
        moved = times(entry, right(total[j, 0:grid, :]))
        slope = slope + moved[:grid]
        rest = rest + moved[grid : grid + 1] + total[j, grid : grid + 1, :]
    sum_ref[0:grid, :] = slope
    sum_ref[grid:, :] = jnp.concatenate(
        [rest, whole_reach, jnp.zeros((VEC - 2, grid), F32)], axis=0
    )


def merged_kernel(level, *refs):
    own_ref, other_ref, own_sum_ref, other_sum_ref, *before, sum_ref, later_ref = refs
    grid = own_ref.shape[1]
    upper = bit(level)

    def put(to_ref, slope, rest, reach):
        to_ref[0:grid, :] = slope
        to_ref[grid:, :] = jnp.concatenate([rest, reach, jnp.zeros((VEC - 2, grid), F32)], axis=0)

    def joined(first_ref, low_ref, high_ref):
        moved = times(first_ref[...], right(high_ref[0:grid, :]))
        slope, rest = moved[:grid], moved[grid : grid + 1] + high_ref[grid : grid + 1, :]
        low, high = low_ref[grid + 1 : grid + 2, :], high_ref[grid + 1 : grid + 2, :]
        put(
            sum_ref, low_ref[0:grid, :] + slope * low,
            low_ref[grid : grid + 1, :] + rest * low, low * high,
        )
        return slope, rest, high

    @pl.when(upper == 0)
    def _():
        slope, rest, high = joined(own_ref, own_sum_ref, other_sum_ref)
        if before:
            old = before[0]
            reach = old[grid + 1 : grid + 2, :]
            slope = old[0:grid, :] + slope * reach
            rest = old[grid : grid + 1, :] + rest * reach
            high = reach * high
        put(later_ref, slope, rest, high)

    @pl.when(upper > 0)
    def _():
        joined(other_ref, other_sum_ref, own_sum_ref)
        if before:
            old = before[0]
            moved = times(other_ref[...], right(old[0:grid, :]))
            put(
                later_ref, moved[:grid], moved[grid : grid + 1] + old[grid : grid + 1, :],
                old[grid + 1 : grid + 2, :],
            )
        else:
            nothing = jnp.zeros((grid, grid), F32)
            put(later_ref, nothing, nothing[0:1], nothing[0:1] + 1.0)


def padded(row):
    return jnp.concatenate([row, jnp.zeros((VEC - 1, row.shape[1]), F32)], axis=0)


def ordered(held, own, other, upper):
    held[0] = own
    held[1] = other
    return after(held[upper], held[1 - upper])


def half_rows(whole_ref, half_ref, core):
    half = half_ref.shape[0] - VEC
    half_ref[0:half, :] = whole_ref[pl.ds(pl.multiple_of(core * half, half), half), :]
    half_ref[half:, :] = whole_ref[2 * half :, :]


def core_kernel(
    own_ref, other_ref, own_v_ref, other_v_ref, one_ref, two_ref, whole_ref, half_ref, held,
):
    grid = own_ref.shape[0]
    one_ref[0:grid, :] = own_ref[...]
    one_ref[grid:, :] = own_v_ref[...]
    two_ref[0:grid, :] = other_ref[...]
    two_ref[grid:, :] = other_v_ref[...]
    whole_ref[...] = ordered(held, one_ref[...], two_ref[...], bit(0))
    half_rows(whole_ref, half_ref, bit(0))


def join(mine_ref, theirs_ref, other_ref):
    half = mine_ref.shape[0] - VEC
    core = bit(0)
    other_ref[pl.ds(pl.multiple_of(core * half, half), half), :] = mine_ref[0:half, :]
    other_ref[pl.ds(pl.multiple_of((1 - core) * half, half), half), :] = theirs_ref[0:half, :]
    other_ref[2 * half :, :] = mine_ref[half:, :]


def halves_kernel(level, own_ref, mine_ref, theirs_ref, whole_ref, half_ref, other_ref, held):
    join(mine_ref, theirs_ref, other_ref)
    whole_ref[...] = ordered(held, own_ref[...], other_ref[...], bit(level))
    half_rows(whole_ref, half_ref, bit(0))


def end_kernel(level, own_ref, mine_ref, theirs_ref, end_ref, other_ref, held):
    grid = own_ref.shape[1]
    upper = bit(level)
    join(mine_ref, theirs_ref, other_ref)
    held[0] = own_ref[...]
    held[1] = other_ref[...]
    later = held.at[1 - upper]
    end_ref[...] = times(held[upper, grid:, :], right(later[:grid, :])) + later[grid:, :]


def starts_kernel(*refs):
    others, (prefix_ref, start_ref, starts_ref, shifts_ref, lead_ref, held) = refs[:4], refs[4:]
    chains, grid = prefix_ref.shape[0], prefix_ref.shape[2]
    top = others[3]
    row = lax.broadcasted_iota(jnp.int32, top.shape, 0)
    column = lax.broadcasted_iota(jnp.int32, top.shape, 1)
    held[...] = jnp.where(bit(3) > 0, top[...], jnp.where(row == column, 1.0, 0.0))
    for level in (2, 1, 0):
        if level == MERGED - 1:
            lead_ref[...] = held[...]

        @pl.when(bit(level) > 0)
        def _():
            held[...] = after(held[...], others[level][...])
    starts_ref[0] = held[:grid, :]
    rows = [held[grid : grid + 1, :]]
    for j in range(1, chains):
        moved = times(held[...], right(prefix_ref[j - 1]))
        starts_ref[j] = moved[:grid]
        rows.append(moved[grid : grid + 1] + start_ref[j : j + 1, :])
    shifts_ref[...] = jnp.concatenate([*rows, jnp.zeros((VEC - chains, grid), F32)], axis=0)


def ahead_kernel(lead_ref, sum_ref, later_ref, ahead_ref, tail_ref):
    grid = lead_ref.shape[1]
    tail = []
    for k, part_ref in enumerate((sum_ref, later_ref)):
        moved = times(lead_ref[...], right(part_ref[0:grid, :]))
        ahead_ref[k] = moved[:grid]
        tail.append(moved[grid : grid + 1] + part_ref[grid : grid + 1, :])
        tail.append(part_ref[grid + 1 : grid + 2, :])
    tail_ref[...] = jnp.concatenate([*tail, jnp.zeros((VEC - 4, grid), F32)], axis=0)


def send_kernel(end_ref, group_ref, ahead_ref, tail_ref, state_ref, send_ref):
    state = jnp.where(bit(5) > 0, end_ref[...], 0.0)
    state = jnp.where(bit(4) > 0, advance(state, group_ref[...]), state)
    state_ref[...] = state
    v = times(state, right(ahead_ref[0]))[0:1] + tail_ref[0:1, :]
    d = tail_ref[1:2, :]
    send_ref[...] = jnp.broadcast_to(jnp.concatenate([d, v], axis=1)[None], send_ref.shape)


def advance(state, whole):
    grid = whole.shape[1]
    return times(state, right(whole[:grid])) + whole[grid : grid + 1]


def final_kernel(
    state_ref, starts_ref, shifts_ref, ahead_ref, tail_ref, drive_ref, gains_ref, smooth_ref,
    transition_ref, filtered_ref, weight_ref, value_ref, found, scan_d, scan_v,
):
    chains = starts_ref.shape[0]
    frames = drive_ref.shape[0]
    part = lax.axis_index("y")
    step = right(transition_ref[...].T)
    state = state_ref[...]
    rows = [times(state, right(starts_ref[j]))[0:1] for j in range(chains)]
    now = jnp.concatenate(rows, axis=0) + shifts_ref[0:chains, :]
    for t in range(SUB):
        keep = 1.0 - each(gains_ref, t, chains)
        now = times(now, step) * keep + each(drive_ref, t, chains)
        for j in range(chains):
            found[SUB * j + t : SUB * j + t + 1, :] = now[j : j + 1]
    weight = closed(smooth_ref)
    value = found[...] - weight * times(found[...], step)
    d, v = weight[frames - 1 : frames], value[frames - 1 : frames]
    scan_d[frames - 1 : frames, :] = d
    scan_v[frames - 1 : frames, :] = v
    for t in range(frames - 2, -1, -1):
        v = weight[t : t + 1] * v + value[t : t + 1]
        d = weight[t : t + 1] * d
        scan_d[t : t + 1, :] = d
        scan_v[t : t + 1, :] = v
    share = filtered_ref.shape[0]
    mine = pl.ds(pl.multiple_of(part * share, share), share)
    filtered_ref[...] = found[mine, :]
    later = times(state, right(ahead_ref[1]))[0:1] + tail_ref[2:3, :]
    weight_ref[...] = scan_d[mine, :] * tail_ref[3:4, :]
    value_ref[...] = scan_d[mine, :] * later + scan_v[mine, :]


def smooth_kernel(got_ref, weight_ref, value_ref, smoothed_ref):
    blocks = got_ref.shape[0]
    grid = weight_ref.shape[1]
    here = lax.axis_index(TM) >> MERGED
    row = lax.broadcasted_iota(jnp.int32, (blocks, grid), 0)
    d = jnp.where(row > here, got_ref[:, :grid], 1.0)
    v = jnp.where(row > here, got_ref[:, grid:], 0.0)
    later = jnp.zeros((1, grid), F32)
    for k in range(blocks - 1, -1, -1):
        later = d[k : k + 1] * later + v[k : k + 1]
    smoothed_ref[...] = weight_ref[...] * later + value_ref[...]


def shape(*dims):
    return jax.ShapeDtypeStruct(dims, F32)


V = pl.BlockSpec(memory_space=pltpu.VMEM)
ROOM = pltpu.CompilerParams(vmem_limit_bytes=12 << 20)


def call(kernel, ins, outs, out_shape, scratch=()):
    return pl.pallas_call(
        kernel, in_specs=ins, out_specs=outs, out_shape=out_shape,
        scratch_shapes=list(scratch), compiler_params=ROOM,
    )


def on_device(
    features, w_in, b_in, output_weight, final_offset_entries, transition, gains, smooth_gains
):
    frames, grid = gains.shape
    chains = frames // SUB
    rows = grid + VEC
    among = TM[: len(TM) - MERGED]
    blocks = lax.axis_size(among)
    parts = lax.axis_size("y")
    H = pl.BlockSpec(memory_space=pltpu.HBM)
    units = w_in.shape[1]
    matrix, stack = shape(grid, grid), shape(chains, grid, grid)
    arrays = (features, w_in, b_in[None], output_weight, gains, transition)
    partial, early = call(
        network_kernel, [H] * 6, [V, V], [shape(frames, grid), stack],
        [
            pltpu.VMEM(features.shape, BF16), pltpu.VMEM(w_in.shape, BF16),
            pltpu.VMEM((1, units), F32), pltpu.VMEM(output_weight.shape, BF16),
            pltpu.VMEM(gains.shape, F32), pltpu.VMEM(transition.shape, F32),
            pltpu.VMEM((frames, units), F32), pltpu.SemaphoreType.DMA((8 + 5,)),
        ],
    )(*(pltpu.with_memory_space_constraint(a, pltpu.HBM) for a in arrays))

    def moved(a, axis, to):
        pairs = [(k, to(k)) for k in range(lax.axis_size(axis))]
        return lax.ppermute(a, axis, [(k, n) for k, n in pairs if n is not None])

    partials = [partial] + [
        moved(partial, "y", lambda k: (k + s) % parts) for s in range(1, parts)
    ]
    block, chain, prefix = call(block_kernel, [V] * 3, [V] * 3, [matrix, stack, stack])(
        gains, transition, early
    )
    *partials, block = lax.optimization_barrier((*partials, block))
    other_block = moved(block, "c", lambda k: 1 - k)
    ended, drive, start = call(
        response_kernel, [V] * 8, [V] * 3, [shape(VEC, grid), shape(frames, grid), shape(VEC, grid)],
    )(*partials, final_offset_entries[None], gains, transition, chain)
    ended, other_block = lax.optimization_barrier((ended, other_block))

    big, small = shape(rows, grid), shape(grid // 2 + VEC, grid)
    held = [pltpu.VMEM((2, rows, grid), F32)]

    ways = [
        ("c", lambda k: 1 - k), (Z, lambda k: k ^ 1), (Z, lambda k: k ^ 3),
        (Z, lambda k: 7 - k), ("x", lambda k: k ^ 1), ("x", lambda k: 3 - k),
    ]
    one, two, whole, half = call(
        core_kernel, [V] * 4, [V] * 4, [big, big, big, small], held
    )(block, other_block, ended, moved(ended, *ways[0]))
    wholes, others = [one], [two]
    for level in (1, 2, 3):
        wholes.append(whole)
        mine = moved(half, *ways[level])
        if level == 2:
            drive, _ = lax.optimization_barrier((drive, half))
            total = call(
                summary_kernel, [V] * 6, V, big,
                [pltpu.VMEM((chains, rows, grid), F32)] * 2 + [pltpu.VMEM((frames, grid), F32)],
            )(gains, smooth_gains, transition, drive, prefix, start)
            mine, total = lax.optimization_barrier((mine, total))
        if level == 3:
            total, later = call(
                functools.partial(merged_kernel, 0), [V] * 4, [V, V], [big, big]
            )(wholes[0], others[0], total, moved(total, *ways[0]))
            mine, total = lax.optimization_barrier((mine, total))
        theirs = moved(mine, *ways[0])
        whole, half, other = call(
            functools.partial(halves_kernel, level), [V] * 3, [V] * 3, [big, small, big], held
        )(whole, mine, theirs)
        others.append(other)
    mine = moved(half, *ways[4])
    starts, shifts, lead = call(
        starts_kernel, [V] * 6, [V] * 3, [stack, shape(VEC, grid), big],
        [pltpu.VMEM((rows, grid), F32)],
    )(*others, prefix, start)
    mine, lead = lax.optimization_barrier((mine, lead))
    if MERGED > 1:
        total, _ = lax.optimization_barrier((total, half))
        total, later = call(
            functools.partial(merged_kernel, 1), [V] * 5, [V, V], [big, big]
        )(wholes[1], others[1], total, moved(total, *ways[1]), later)
    theirs = moved(mine, *ways[0])
    end, group = call(
        functools.partial(end_kernel, 4), [V] * 3, [V, V], [shape(VEC, grid), big], held
    )(whole, mine, theirs)
    end = moved(end, *ways[5])
    ahead, tail = call(ahead_kernel, [V] * 3, [V, V], [shape(2, grid, grid), shape(VEC, grid)])(
        lead, total, later
    )

    share = frames // parts
    state, send = call(
        send_kernel, [V] * 4, [V, V], [shape(VEC, grid), shape(blocks, 1, 2 * grid)]
    )(end, group, ahead, tail)
    got = lax.all_to_all(send, among, 0, 0, tiled=True)[:, 0]
    filtered, weight, value = call(
        final_kernel, [V] * 9, [V] * 3, [shape(share, grid)] * 3,
        [pltpu.VMEM((frames, grid), F32)] * 3,
    )(state, starts, shifts, ahead, tail, drive, gains, smooth_gains, transition)
    smoothed = call(smooth_kernel, [V, V, V], V, shape(share, grid))(
        got, weight, value
    )
    return filtered, smoothed


def solution(mesh):
    torus = Mesh(mesh.devices.reshape(4, 4, 2, 2, mesh.shape["mp"]), ("x", "q", "k", "c", "y"))
    return jax.shard_map(
        on_device,
        mesh=torus,
        in_specs=(
            P(TM, None), P(None, "y"), P("y"), P("y", None), P(), P(), P(TM, None), P(TM, None),
        ),
        out_specs=(P((*TM, "y"), None), P((*TM, "y"), None)),
        check_vma=False,
    )
```
